32 devices in a mesh: chain: 8 (over z, y), col: 4 (over x, core).
Axes of the slice: x: 2, y: 2, z: 4, core: 2. Of those that a mesh axis runs over, the one named last changes fastest.
Arguments:
- rhs: bfloat16 [4, 8, 32, 128], P(None, 'chain'), may hold values from -6 to 6
- pattern: int32 [4, 8, 24], P(None, 'chain', 'col'), may hold values from 0 to 31, as said below
- factor: bfloat16 [4, 8, 24, 128, 128], P(None, 'chain', 'col'), may hold values from -0.1875 to 0.1875
- inverse: bfloat16 [4, 8, 128, 128], P(None, 'chain'), as said below
- level_size: int32 [6], replicated, may hold values from 1 to 8, 32 in all
Outputs:
- half_solved: bfloat16 [4, 8, 32, 128], P(None, 'chain')
- solved: bfloat16 [4, 8, 32, 128], P(None, 'chain')
The draws below stay inside these ranges and needn't reach their ends.
Inputs may be any that keep to these rules, and one draw needn't show every extreme that they name: Among the pattern entries held by one index of chain and one index of col (all 4 of its block rows), at most 3 name block rows on any one index of chain (block row mod 8); in every such group exactly 3 name block rows on one index of chain that is common to all groups of that index of col. A block row may name a block row more than once. `inverse`: each block is lower triangular with a diagonal between 0.3 and 2.
All inputs are finite; a program needn't handle non-finite values.
Results may differ from the reference program's by a relative error of at most 0.013.
Values may be sent and summed in bfloat16 or wider, within the bound.
A program may use at most 64 MiB of HBM per device.

```python
import math
import jax
import jax.numpy as jnp
import numpy as np
from jax import lax

BLOCK = 128
NNZ = 24
PROBES = 32
ROWS_DEV = 4
LEVELS = 6
BLOCK_ROWS = 32
CAP = 3
N_CHAIN = 8
N_COL = 4


def draw_pattern(key, part):
    entries = NNZ // N_COL
    count = ROWS_DEV * entries
    runs = (count + CAP - 1) // CAP
    key_first = jax.random.fold_in(key, 21)
    key_perm = jax.random.fold_in(key, 22)
    key_base = jax.random.fold_in(key, 23)
    first = jax.random.randint(key_first, (N_COL,), 0, N_CHAIN, dtype=jnp.int32)
    group_keys = jax.random.split(key_perm, N_CHAIN * N_COL)
    others = jax.vmap(lambda single: jax.random.permutation(single, N_CHAIN - 1))(group_keys)
    others = others.astype(jnp.int32).reshape(N_CHAIN, N_COL, N_CHAIN - 1)
    firsts = jnp.broadcast_to(first[None, :, None], (N_CHAIN, N_COL, 1))
    order = jnp.concatenate([firsts, (firsts + 1 + others) % N_CHAIN], axis=2)
    positions = jnp.arange(count, dtype=jnp.int32)
    run_ids = positions // CAP
    lane = order[:, :, run_ids]
    base = jax.random.randint(key_base, (N_CHAIN, N_COL, runs), 0, ROWS_DEV, dtype=jnp.int32)
    quotient = (base[:, :, run_ids] + (positions % CAP)[None, None, :]) % ROWS_DEV
    column = quotient * N_CHAIN + lane
    column = column.reshape(N_CHAIN, N_COL, ROWS_DEV, entries).transpose(2, 0, 1, 3)
    return column.reshape(ROWS_DEV, N_CHAIN, NNZ).astype(jnp.int32)


def draw_inverse(key, part):
    key_diag = jax.random.fold_in(key, 11)
    key_low = jax.random.fold_in(key, 12)
    diagonal = jax.random.uniform(key_diag, (ROWS_DEV, N_CHAIN, BLOCK), jnp.float32, 0.5, 1.5)
    lower = jax.random.normal(key_low, (ROWS_DEV, N_CHAIN, BLOCK, BLOCK), jnp.float32)
    lower = jnp.tril(lower, -1) * (0.6 / jnp.sqrt(BLOCK * 1.0))
    eye = jnp.eye(BLOCK, dtype=jnp.float32)
    return (lower + diagonal[..., None] * eye).astype(jnp.bfloat16)


def level_of(key, extent, shards, smallest, largest):
    def one(axis_at, blocks):
        steps = jax.random.uniform(jax.random.fold_in(jax.random.fold_in(key, 6), axis_at), (blocks,), jnp.float32, smallest / len(shards), largest / len(shards))
        return jnp.repeat(jnp.exp(steps), extent[axis_at] // blocks).reshape((-1,) + (1,) * (len(extent) - axis_at - 1))

    level = one(*shards[0])
    for cut in shards[1:]:
        level = level * one(*cut)
    return level


def split_up(number_of, total, bound, lean):
    weights = [(1 << 20) // math.isqrt(grade ** lean) + 1 for grade in range(2, number_of + 1)]
    spare, counts = total - bound - (number_of - 1), [1] * (number_of - 1)
    while spare > 0:
        movable = [i for i in range(number_of - 1) if counts[i] < bound]
        whole, remaining = sum([weights[i] for i in movable]), spare
        for i in movable:
            extra = min(bound - counts[i], max(1, remaining * weights[i] // whole), spare)
            counts[i] = counts[i] + extra
            spare = spare - extra
    return np.array([bound] + counts)


def uneven(own_key, amount, total, most, slope):
    if amount == 2:
        one = jax.random.randint(own_key, (), max(1, total - most), min(most, total - 1) + 1)
        return jnp.stack([one, total - one])
    sizes = jnp.asarray(split_up(amount, total, most, slope), jnp.int32)
    couples = (amount - 1) // 2
    donor, taker = sizes[1:1 + 2 * couples:2], sizes[2:2 + 2 * couples:2]
    margin = jnp.minimum(donor - 1, most - taker)
    passed = jax.random.randint(jax.random.fold_in(own_key, 1), (couples,), 0, 1 << 20) % (margin + 1)
    sizes = sizes.at[1:1 + 2 * couples:2].set(donor - passed).at[2:2 + 2 * couples:2].set(taker + passed)
    return sizes[jax.random.permutation(jax.random.fold_in(own_key, 2), amount)]


def scatter_about(stream_key, shape, width, limit, cuts=(), held_as=jnp.bfloat16):
    result = width * jax.random.normal(stream_key, shape, jnp.float32)
    if cuts:
        result = result * level_of(stream_key, shape, cuts, -0.22, 0.18)
    return jnp.clip(result, -limit, limit).astype(held_as)


def setup_inputs(seed: int = 0) -> dict:
    seeds = jax.random.split(jax.random.key(seed), 6)
    rhs = scatter_about(seeds[0], (ROWS_DEV, N_CHAIN, PROBES, BLOCK), 1.0, 6.0, ((1, 8),))
    pattern = draw_pattern(jax.random.fold_in(seeds[5], 71), 0)
    factor = scatter_about(seeds[2], (ROWS_DEV, N_CHAIN, NNZ, BLOCK, BLOCK), (BLOCK * NNZ // 3) ** -0.5, 0.1875, ((1, 8), (2, 4)))
    inverse = draw_inverse(jax.random.fold_in(seeds[5], 71), 0)
    level_size = uneven(seeds[4], LEVELS, BLOCK_ROWS, N_CHAIN, 0).astype(jnp.int32)
    return {"rhs": rhs, "pattern": pattern, "factor": factor, "inverse": inverse, "level_size": level_size}


def level_index(positions, ends):
    return jnp.sum((positions[..., None] >= ends).astype(jnp.int32), axis=-1)


def reference(rhs, pattern, factor, inverse, level_size):
    total = ROWS_DEV * N_CHAIN
    right = rhs.reshape(total, PROBES, BLOCK)
    columns = pattern.reshape(total, NNZ).astype(jnp.int32)
    blocks = factor.reshape(total, NNZ, BLOCK, BLOCK)
    inverse_rows = inverse.reshape(total, BLOCK, BLOCK)
    ends = jnp.cumsum(level_size).astype(jnp.int32)
    row_level = level_index(jnp.arange(total, dtype=jnp.int32), ends)
    keep = level_index(columns, ends) < row_level[:, None]

    def forward(store, row_id):
        chosen = jnp.where(keep[row_id][:, None, None], store[columns[row_id]], 0).astype(jnp.float32)
        partial_value = jnp.einsum("jpb,jcb->pc", chosen, blocks[row_id].astype(jnp.float32), precision=lax.Precision.HIGHEST)
        rest = (right[row_id].astype(jnp.float32) - partial_value).astype(jnp.bfloat16)
        segment = jnp.dot(rest, inverse_rows[row_id].T, preferred_element_type=jnp.float32).astype(jnp.bfloat16)
        return store.at[row_id].set(segment), None

    store, _ = lax.scan(forward, jnp.zeros((total, PROBES, BLOCK), jnp.bfloat16), jnp.arange(total, dtype=jnp.int32))

    def backward(accum, row_id):
        rest = (store[row_id].astype(jnp.float32) - accum[row_id]).astype(jnp.bfloat16)
        segment = jnp.dot(rest, inverse_rows[row_id], preferred_element_type=jnp.float32).astype(jnp.bfloat16)
        terms = jnp.einsum("pc,jcb->jpb", segment.astype(jnp.float32), blocks[row_id].astype(jnp.float32), precision=lax.Precision.HIGHEST)
        terms = jnp.where(keep[row_id][:, None, None], terms, 0.0)
        accum = accum.at[columns[row_id]].add(terms)
        return accum, segment

    _, solved = lax.scan(backward, jnp.zeros((total, PROBES, BLOCK), jnp.float32), jnp.arange(total, dtype=jnp.int32), reverse=True)
    return store.reshape(rhs.shape), solved.reshape(rhs.shape)
```

```python
import functools

import jax
import jax.numpy as jnp
from jax import lax
from jax.experimental import pallas as pl
from jax.experimental.pallas import tpu as pltpu
from jax.sharding import PartitionSpec as P

MESH = pl.DeviceIdType.MESH
F32 = jnp.float32
BF16 = jnp.bfloat16


def kernel(
    n_chain,
    n_col,
    levels,
    rhs_hbm,
    pat_hbm,
    fac_hbm,
    inv_hbm,
    size_ref,
    half_out,
    solved_out,
    rhs_v,
    inv_v,
    fac_v,
    pat_v,
    pat_s,
    code_s,
    gn,
    gt,
    base,
    store,
    frx,
    btx,
    brx,
    acc,
    half_lv,
    sol_lv,
    in_sem,
    pat_sem,
    f_send,
    f_recv,
    b_send,
    b_recv,
    p_send,
    p_recv,
    t_send,
    t_recv,
    n_send,
    n_recv,
    o_send,
    o_recv,
):
    rows = rhs_v.shape[0]
    probes = rhs_v.shape[2]
    width = rhs_v.shape[3]
    entries = fac_v.shape[2]
    total = 2 * entries
    groups = n_col // 2
    workers = n_chain * groups
    me = lax.axis_index("chain")
    k = lax.axis_index("col")
    group = lax.div(k, 2)
    is_worker = lax.rem(k, 2) == 1
    sibling = {"col": k + 1 - 2 * lax.rem(k, 2)}

    load_rhs = pltpu.make_async_copy(rhs_hbm, rhs_v, in_sem.at[0])
    load_inv = pltpu.make_async_copy(inv_hbm, inv_v, in_sem.at[1])
    load_fac = pltpu.make_async_copy(fac_hbm, fac_v, in_sem.at[2])
    load_rhs.start()
    load_inv.start()
    load_fac.start()

    barrier = pltpu.get_barrier_semaphore()

    def flip(mask):
        if n_chain & (n_chain - 1):
            return lax.rem(me + mask, n_chain)
        out = me
        bit = 1
        while bit < n_chain:
            if mask & bit:
                out = out + bit - 2 * bit * lax.rem(lax.div(me, bit), 2)
            bit *= 2
        return out

    lanes = [flip(mask) for mask in range(n_chain)]
    columns = [2 * lax.rem(group + g, groups) + 1 for g in range(groups)]
    peers = [
        (lanes[d], columns[g])
        for g in reversed(range(groups))
        for d in reversed(range(n_chain))
        if d or g
    ]

    pat_copy = pltpu.make_async_remote_copy(
        src_ref=pat_hbm,
        dst_ref=pat_v,
        send_sem=p_send,
        recv_sem=p_recv,
        device_id=sibling,
        device_id_type=MESH,
    )
    gt_copy = pltpu.make_async_remote_copy(
        src_ref=gt.at[0],
        dst_ref=gt.at[1],
        send_sem=t_send,
        recv_sem=t_recv,
        device_id=sibling,
        device_id_type=MESH,
    )
    gn_copy = pltpu.make_async_remote_copy(
        src_ref=gn.at[0],
        dst_ref=gn.at[1],
        send_sem=n_send,
        recv_sem=n_recv,
        device_id=sibling,
        device_id_type=MESH,
    )
    half_copy = pltpu.make_async_remote_copy(
        src_ref=half_out,
        dst_ref=half_out,
        send_sem=o_send.at[0],
        recv_sem=o_recv.at[0],
        device_id=sibling,
        device_id_type=MESH,
    )
    solved_copy = pltpu.make_async_remote_copy(
        src_ref=solved_out,
        dst_ref=solved_out,
        send_sem=o_send.at[1],
        recv_sem=o_recv.at[1],
        device_id=sibling,
        device_id_type=MESH,
    )

    def fold():
        for row in range(rows):
            for j in range(entries):
                block = jnp.dot(inv_v[row, 0], fac_v[row, 0, j], preferred_element_type=F32)
                gn[0, row, j] = block.astype(BF16)
                gt[0, row, j] = block.T.astype(BF16)

    @pl.when(jnp.logical_not(is_worker))
    def _():
        pl.semaphore_signal(barrier, inc=1, device_id=sibling, device_id_type=MESH)
        pl.semaphore_wait(barrier, 1)
        pat_copy.start()
        load_rhs.wait()
        load_inv.wait()
        load_fac.wait()
        fold()
        gt_copy.start()
        gn_copy.start()
        half_copy.wait_recv()
        solved_copy.wait_recv()
        pat_copy.wait_send()
        gt_copy.wait_send()
        gn_copy.wait_send()

    @pl.when(is_worker)
    def _():
        for chain, col in peers:
            pl.semaphore_signal(barrier, inc=1, device_id=(chain, col), device_id_type=MESH)
        pl.semaphore_signal(barrier, inc=1, device_id=sibling, device_id_type=MESH)
        own_pat = pltpu.make_async_copy(pat_hbm, pat_s.at[0], pat_sem.at[0])
        own_pat.start()

        ends = []
        running = jnp.int32(0)
        for level in range(levels):
            running = running + size_ref[level]
            ends.append(running)

        def level_of(position):
            found = jnp.int32(0)
            for end in ends[:-1]:
                found = found + (position >= end).astype(jnp.int32)
            return found

        own_level = [level_of(row * n_chain + me) for row in range(rows)]
        slot = []
        live = []
        for level in range(levels):
            here = jnp.int32(0)
            count = jnp.int32(0)
            for row in range(rows):
                match = own_level[row] == level
                here = jnp.where(match, row, here)
                count = count + match.astype(jnp.int32)
            slot.append(here)
            live.append(count > 0)

        load_rhs.wait()
        load_inv.wait()

        def times_inverse_t(row):
            return lax.dot_general(
                rhs_v[row, 0], inv_v[row, 0], (((1,), (1,)), ((), ())), preferred_element_type=F32
            )

        first = times_inverse_t(0)
        frx[0, me] = first.astype(BF16)
        pl.semaphore_wait(barrier, len(peers) + 1)

        def send(source, target, send_sem, recv_sem, chain, col):
            pltpu.make_async_remote_copy(
                src_ref=source,
                dst_ref=target,
                send_sem=send_sem,
                recv_sem=recv_sem,
                device_id=(chain, col),
                device_id_type=MESH,
            ).start()

        def drain(ref, sem, count):
            part = ref.at[pl.ds(0, count)]
            pltpu.make_async_copy(part, part, sem).wait()

        for d in reversed(range(1, n_chain)):
            send(frx.at[0, me], frx.at[0, me], f_send.at[0], f_recv.at[0], lanes[d], k)

        load_fac.wait()
        fold()
        keep = (group == 0).astype(F32)
        base[0] = first * keep
        for row in range(1, rows):
            base[row] = times_inverse_t(row) * keep
        store[pl.ds(n_chain, (levels - 1) * n_chain)] = jnp.zeros(
            ((levels - 1) * n_chain, probes, width), BF16
        )
        acc[...] = jnp.zeros_like(acc)
        own_pat.wait()
        pat_copy.wait_recv()
        other_pat = pltpu.make_async_copy(pat_v, pat_s.at[1], pat_sem.at[1])
        other_pat.start()
        other_pat.wait()
        for row in range(rows):
            for who in range(2):
                for j in range(entries):
                    target = pat_s[who, row, 0, j]
                    code_s[row, who * entries + j] = level_of(target) * n_chain + lax.rem(
                        target, n_chain
                    )
        gt_copy.wait_recv()

        mine = group * n_chain + me
        for level in range(1, levels):
            at = (level - 1) * n_chain
            if level == 1:
                drain(frx.at[0], f_recv.at[0], n_chain - 1)
                store[pl.ds(0, n_chain)] = frx[0, pl.ds(0, n_chain)]
            else:
                drain(frx.at[level - 1], f_recv.at[level - 1], workers - 1)
                for b in range(n_chain):
                    sums = frx[level - 1, b].astype(F32)
                    for g in range(1, groups):
                        sums = sums + frx[level - 1, g * n_chain + b].astype(F32)
                    store[at + b] = sums.astype(BF16)
            row = slot[level]
            left = jnp.concatenate([store[code_s[row, j]] for j in range(total)], axis=1)
            right = jnp.concatenate(
                [gt[who, row].reshape(entries * width, width) for who in range(2)], axis=0
            )
            sums = jnp.dot(left, right, preferred_element_type=F32)
            frx[level, mine] = (base[row] - sums).astype(BF16)
            for chain, col in peers:
                send(
                    frx.at[level, mine],
                    frx.at[level, mine],
                    f_send.at[level],
                    f_recv.at[level],
                    chain,
                    col,
                )
            half_lv[level - 1] = store[at + me]

        last = levels - 1
        drain(frx.at[last], f_recv.at[last], workers - 1)
        partner = frx[last, me].astype(F32)
        for g in range(1, groups):
            partner = partner + frx[last, g * n_chain + me].astype(F32)
        value = partner.astype(BF16)
        half_lv[last] = value
        gn_copy.wait_recv()

        for level in reversed(range(1, levels)):
            row = slot[level]
            clean = jnp.where(live[level], value.astype(F32), 0.0).astype(BF16)
            terms = []
            for j in range(0, total, 2):
                pair = jnp.concatenate(
                    [gn[jj // entries, row, jj % entries] for jj in (j, j + 1)], axis=1
                )
                both = jnp.dot(clean, pair, preferred_element_type=F32)
                terms += [both[:, :width], both[:, width:]]
            codes = [code_s[row, j] for j in range(total)]

            def gathered(target, b):
                sums = acc[target, b]
                for j in range(total):
                    sums = sums + jnp.where(codes[j] == target * n_chain + b, terms[j], 0.0)
                return sums

            t = level - 1
            for b in range(n_chain):
                btx[t, b] = gathered(t, b).astype(BF16)
            brx[t, mine] = btx[t, me]
            for chain, col in peers:
                send(btx.at[t, chain], brx.at[t, mine], b_send.at[t], b_recv.at[t], chain, col)
            sol_lv[level] = jnp.dot(
                value, inv_v[row, 0], preferred_element_type=F32
            ).astype(BF16)
            if level == last:
                for r in range(rows):
                    half_out[r, 0] = half_lv[own_level[r]]
                half_copy.start()
            for target in range(t):
                for b in range(n_chain):
                    acc[target, b] = gathered(target, b)
            drain(brx.at[t], b_recv.at[t], workers - 1)
            sums = brx[t, 0].astype(F32)
            for w in range(1, workers):
                sums = sums + brx[t, w].astype(F32)
            value = (half_lv[t].astype(F32) - sums).astype(BF16)

        sol_lv[0] = jnp.dot(value, inv_v[slot[0], 0], preferred_element_type=F32).astype(BF16)
        for r in range(rows):
            solved_out[r, 0] = sol_lv[own_level[r]]
        solved_copy.start()
        drain(frx.at[0], f_send.at[0], n_chain - 1)
        for level in range(1, levels):
            drain(frx.at[level], f_send.at[level], workers - 1)
        for level in range(levels - 1):
            drain(brx.at[level], b_send.at[level], workers - 1)
        half_copy.wait_send()
        solved_copy.wait_send()


def per_device(n_chain, n_col, rhs, pattern, factor, inverse, level_size):
    rows, _, probes, width = rhs.shape
    entries = factor.shape[2]
    levels = level_size.shape[0]
    total = 2 * entries
    workers = n_chain * (n_col // 2)
    dma = pltpu.SemaphoreType.DMA
    vmem = pl.BlockSpec(memory_space=pltpu.VMEM)
    hbm = pl.BlockSpec(memory_space=pl.ANY)
    out = pltpu.VMEM(rhs.shape, rhs.dtype)
    return pl.pallas_call(
        functools.partial(kernel, n_chain, n_col, levels),
        out_shape=(out, out),
        in_specs=[hbm, hbm, hbm, hbm, pl.BlockSpec(memory_space=pltpu.SMEM)],
        out_specs=(vmem, vmem),
        scratch_shapes=[
            pltpu.VMEM(rhs.shape, BF16),
            pltpu.VMEM(inverse.shape, BF16),
            pltpu.VMEM(factor.shape, BF16),
            pltpu.VMEM((rows, 1, entries), jnp.int32),
            pltpu.SMEM((2, rows, 1, entries), jnp.int32),
            pltpu.SMEM((rows, total), jnp.int32),
            pltpu.VMEM((2, rows, entries, width, width), BF16),
            pltpu.VMEM((2, rows, entries, width, width), BF16),
            pltpu.VMEM((rows, probes, width), F32),
            pltpu.VMEM((levels * n_chain, probes, width), BF16),
            pltpu.VMEM((levels, workers, probes, width), BF16),
            pltpu.VMEM((levels, n_chain, probes, width), BF16),
            pltpu.VMEM((levels, workers, probes, width), BF16),
            pltpu.VMEM((levels, n_chain, probes, width), F32),
            pltpu.VMEM((levels, probes, width), BF16),
            pltpu.VMEM((levels, probes, width), BF16),
            dma((3,)),
            dma((2,)),
            dma((levels,)),
            dma((levels,)),
            dma((levels,)),
            dma((levels,)),
            dma,
            dma,
            dma,
            dma,
            dma,
            dma,
            dma((2,)),
            dma((2,)),
        ],
        compiler_params=pltpu.CompilerParams(
            collective_id=0, has_side_effects=True, vmem_limit_bytes=48 * 1024 * 1024
        ),
    )(rhs, pattern, factor, inverse, level_size)


def solution(mesh):
    return jax.shard_map(
        functools.partial(per_device, mesh.shape["chain"], mesh.shape["col"]),
        mesh=mesh,
        in_specs=(
            P(None, "chain", None, None),
            P(None, "chain", "col"),
            P(None, "chain", "col", None, None),
            P(None, "chain", None, None),
            P(),
        ),
        out_specs=(P(None, "chain", None, None), P(None, "chain", None, None)),
        check_vma=False,
    )
```

```python
import functools

import jax
import jax.numpy as jnp
from jax import lax
from jax.experimental import pallas as pl
from jax.experimental.pallas import tpu as pltpu
from jax.sharding import PartitionSpec as P

MESH = pl.DeviceIdType.MESH
F32 = jnp.float32
BF16 = jnp.bfloat16
STEP = 16


def loop(count, body):
    if count <= 8:
        for i in range(count):
            body(i)
    else:
        lax.fori_loop(0, count, lambda i, carry: (body(i), carry)[1], 0)


def tree(parts):
    while len(parts) > 1:
        parts = [a + b for a, b in zip(parts[::2], parts[1::2])] + parts[len(parts) & ~1 :]
    return parts[0]


def kernel(
    n_chain,
    n_col,
    levels,
    rhs_hbm,
    pat_hbm,
    fac_hbm,
    inv_hbm,
    size_ref,
    half_out,
    solved_out,
    rhs_v,
    inv_v,
    fac_v,
    pat_v,
    pat_s,
    code_s,
    blocks,
    dense,
    dense_t,
    base,
    store,
    frx,
    btx,
    brx,
    acc,
    terms,
    half_lv,
    sol_lv,
    in_sem,
    pat_sem,
    f_send,
    f_recv,
    b_send,
    b_recv,
    p_send,
    p_recv,
    s_send,
    s_recv,
    w_send,
    w_recv,
    x_send,
    x_recv,
    o_send,
    o_recv,
):
    rows = rhs_v.shape[0]
    width = rhs_v.shape[3]
    entries = fac_v.shape[2]
    groups = n_col // 2
    last = levels - 1
    first_full = levels - 2
    me = lax.axis_index("chain")
    k = lax.axis_index("col")
    group = lax.div(k, 2)
    is_worker = lax.rem(k, 2) == 1
    sibling = (me, k + 1 - 2 * lax.rem(k, 2))

    load_rhs = pltpu.make_async_copy(rhs_hbm, rhs_v, in_sem.at[0])
    load_inv = pltpu.make_async_copy(inv_hbm, inv_v, in_sem.at[1])
    load_fac = pltpu.make_async_copy(fac_hbm, fac_v, in_sem.at[2])
    load_rhs.start()
    load_inv.start()
    load_fac.start()

    barrier = pltpu.get_barrier_semaphore()

    def flip(mask):
        out = me
        bit = 1
        while bit < n_chain:
            if mask & bit:
                out = out + bit - 2 * bit * lax.rem(lax.div(me, bit), 2)
            bit *= 2
        return out

    lanes = [flip(mask) for mask in range(n_chain)]
    columns = [2 * lax.rem(group + g, groups) + 1 for g in range(groups)]
    chain_order = sorted(range(1, n_chain), key=lambda d: -((d >> 1) + (d & 1)))
    peers = sorted(
        [(d, g) for d in range(n_chain) for g in range(groups) if d or g],
        key=lambda p: -((p[0] >> 1) + (p[0] & 1) + p[1]),
    )

    def remote(source, target, send_sem, recv_sem, device):
        return pltpu.make_async_remote_copy(
            src_ref=source,
            dst_ref=target,
            send_sem=send_sem,
            recv_sem=recv_sem,
            device_id=device,
            device_id_type=MESH,
        )

    def to_group(g):
        return (me, columns[g])

    def pat_to(which, device):
        return remote(pat_hbm, pat_v.at[which], p_send.at[which], p_recv.at[which], device)

    def to_sibling(row):
        return remote(
            blocks.at[0, row], blocks.at[1, row], s_send.at[row], s_recv.at[row], sibling
        )

    def to_helper(row):
        return remote(
            blocks.at[0, row], blocks.at[1, row], w_send.at[row], w_recv.at[row], sibling
        )

    def across(g, own, row):
        which = 2 * g + (0 if own == 1 else 1)
        return remote(
            blocks.at[own, row],
            blocks.at[which, row],
            x_send.at[which, row],
            x_recv.at[which, row],
            to_group(g),
        )

    def out_copy(i, ref):
        return remote(ref, ref, o_send.at[i], o_recv.at[i], sibling)

    def fold(row):
        for j in range(0, entries):
            block = jnp.dot(inv_v[row, 0], fac_v[row, 0, j], preferred_element_type=F32)
            blocks[0, row, j] = block.astype(BF16)

    @pl.when(jnp.logical_not(is_worker))
    def _():
        pl.semaphore_signal(barrier, inc=1, device_id=sibling, device_id_type=MESH)
        load_rhs.wait()
        load_inv.wait()
        load_fac.wait()
        fold(0)
        pl.semaphore_wait(barrier, groups)
        pats = [pat_to(1, sibling)] + [pat_to(2 * g + 1, to_group(g)) for g in range(1, groups)]
        for copy in pats:
            copy.start()
        to_sibling(0).start()
        for row in range(1, rows):
            fold(row)
            to_sibling(row).start()
        order = list(reversed(range(rows)))
        half = (rows + 1) // 2
        for part in (order[:half], order[half:]):
            for row in part:
                for g in range(1, groups):
                    across(g, 0, row).start()
            for row in part:
                to_helper(row).wait_recv()
                for g in range(1, groups):
                    across(g, 1, row).start()
        for copy in pats:
            copy.wait_send()
        for row in range(rows):
            to_sibling(row).wait_send()
            for g in range(1, groups):
                across(g, 0, row).wait_send()
                across(g, 1, row).wait_send()
        out_copy(0, half_out).wait_recv()
        out_copy(1, solved_out).wait_recv()

    @pl.when(is_worker)
    def _():
        for d, g in peers:
            pl.semaphore_signal(
                barrier, inc=1, device_id=(lanes[d], columns[g]), device_id_type=MESH
            )
        for g in range(groups):
            pl.semaphore_signal(
                barrier, inc=1, device_id=(me, columns[g] - 1), device_id_type=MESH
            )
        own_pat = pltpu.make_async_copy(pat_hbm, pat_s.at[0], pat_sem.at[0])
        own_pat.start()

        ends = []
        running = jnp.int32(0)
        for level in range(levels):
            running = running + size_ref[level]
            ends.append(running)

        def level_of(position):
            found = jnp.int32(0)
            for end in ends[:-1]:
                found = found + (position >= end).astype(jnp.int32)
            return found

        own_level = [level_of(row * n_chain + me) for row in range(rows)]
        slot = []
        live = []
        for level in range(levels):
            here = jnp.int32(0)
            count = jnp.int32(0)
            for row in range(rows):
                match = own_level[row] == level
                here = jnp.where(match, row, here)
                count = count + match.astype(jnp.int32)
            slot.append(here)
            live.append(count > 0)

        load_rhs.wait()
        load_inv.wait()

        def times_inverse_t(row):
            return lax.dot_general(
                rhs_v[row, 0], inv_v[row, 0], (((1,), (1,)), ((), ())), preferred_element_type=F32
            )

        first = times_inverse_t(0)
        frx[0, 0] = first.astype(BF16)
        pl.semaphore_wait(barrier, n_chain * groups)

        def drain(ref, start, count, sem):
            part = ref.at[pl.ds(start, count)]
            pltpu.make_async_copy(part, part, sem).wait()

        def share(level, whole):
            for d, g in [(d, 0) for d in chain_order] if whole else peers:
                remote(
                    frx.at[level, 0],
                    frx.at[level, g * n_chain + d],
                    f_send.at[level],
                    f_recv.at[level],
                    (lanes[d], columns[g]),
                ).start()

        def is_whole(level):
            return level == 0 or level >= first_full

        def copies(level):
            return (n_chain if is_whole(level) else n_chain * groups) - 1

        def candidates(level):
            return list(range(max(0, rows - levels + level), min(level, rows - 1) + 1))

        def picked(level, which, j, at):
            first_row, *others = candidates(level)
            block = blocks[which, first_row, j, at, :]
            for row in others:
                block = jnp.where(slot[level] == row, blocks[which, row, j, at, :], block)
            return block

        def fill_codes(whiches):
            for which in whiches:
                for row in range(rows):
                    for j in range(entries):
                        target = pat_s[which, row, 0, j]
                        code_s[which, row, j] = level_of(target) * n_chain + lax.rem(
                            target, n_chain
                        )

        def build(level, whiches, add):
            keys = [
                jnp.where(live[level], code_s[w, slot[level], j], -1) - (level - 1) * n_chain
                for w in whiches
                for j in range(entries)
            ]

            def chunk(i, carry):
                at = pl.ds(pl.multiple_of(i * STEP, STEP), STEP)
                found = [picked(level, w, j, at) for w in whiches for j in range(entries)]
                for d in range(n_chain):
                    parts = [
                        jnp.where(key == lanes[d], block, jnp.zeros_like(block))
                        for key, block in zip(keys, found)
                    ]
                    if add:
                        parts.append(dense[level - 1, d, at, :])
                    dense[level - 1, d, at, :] = tree(parts)
                return carry

            lax.fori_loop(0, width // STEP, chunk, 0)

        def turn(level):
            def one(d):
                at = pl.ds(d * width, width)
                dense_t[at, :] = dense[level - 1, d].astype(F32).T.astype(BF16)

            loop(n_chain, one)

        def older(level, whiches):
            sums = None
            for w in whiches:
                for j in range(0, entries, 2):
                    pair = range(j, min(j + 2, entries))
                    left = jnp.concatenate([store[code_s[w, slot[level], i]] for i in pair], axis=1)
                    right = jnp.concatenate(
                        [picked(level, w, i, pl.ds(0, width)) for i in pair], axis=1
                    )
                    term = lax.dot_general(
                        left, right, (((1,), (1,)), ((), ())), preferred_element_type=F32
                    )
                    sums = term if sums is None else sums + term
            return sums

        near = [0, 1]
        far = list(range(2, n_col))
        share(0, True)

        load_fac.wait()
        for row in reversed(range(rows)):
            fold(row)
            to_helper(row).start()
        pats = [pat_to(2 * g, to_group(g)) for g in range(1, groups)]
        for copy in pats:
            copy.start()
        base[0] = first
        for row in range(1, rows):
            base[row] = times_inverse_t(row)
        store[...] = jnp.zeros_like(store)
        acc[...] = jnp.zeros_like(acc)
        own_pat.wait()
        pat_to(1, sibling).wait_recv()
        other_pat = pltpu.make_async_copy(pat_v.at[1], pat_s.at[1], pat_sem.at[1])
        other_pat.start()
        other_pat.wait()
        fill_codes(near)
        for row in range(rows):
            to_sibling(row).wait_recv()
        build(1, near, False)
        turn(1)

        keep = (group == 0).astype(F32)
        for level in range(1, levels):
            whole = is_whole(level)
            before = base[slot[level]]
            if not whole:
                before = before * keep
            if level > 1:
                before = before - older(level, near + far if whole else near)
            drain(frx.at[level - 1], 1, copies(level - 1), f_recv.at[level - 1])
            found = []
            for d in range(n_chain):
                if is_whole(level - 1):
                    found.append(frx[level - 1, d])
                else:
                    parts = [frx[level - 1, g * n_chain + d].astype(F32) for g in range(groups)]
                    found.append(tree(parts).astype(BF16))
            sums = jnp.dot(
                jnp.concatenate(found, axis=1), dense_t[...], preferred_element_type=F32
            )
            value = (before - sums).astype(BF16)
            half_lv[level - 1] = found[0]
            if level == last:
                half_lv[level] = value
                break
            frx[level, 0] = value
            share(level, whole)
            for d in range(n_chain):
                store[(level - 1) * n_chain + lanes[d]] = found[d]
            if level + 1 == first_full:
                moved = []
                for which in far:
                    pat_to(which, sibling).wait_recv()
                    moved.append(
                        pltpu.make_async_copy(pat_v.at[which], pat_s.at[which], pat_sem.at[which])
                    )
                    moved[-1].start()
                for copy in moved:
                    copy.wait()
                fill_codes(far)
            if is_whole(level + 1):
                for which in far:
                    for row in candidates(level + 1):
                        if level + 1 == first_full:
                            remote(
                                blocks.at[which, row],
                                blocks.at[which, row],
                                x_send.at[which, row],
                                x_recv.at[which, row],
                                sibling,
                            ).wait_recv()
            build(level + 1, near + far if is_whole(level + 1) else near, False)
            turn(level + 1)

        arrived = set(candidates(first_full)) | set(candidates(last))
        for level in reversed(range(1, levels)):
            t = level - 1
            for d in reversed(range(0, n_chain, 2)):
                pair = jnp.concatenate([dense[t, d], dense[t, d + 1]], axis=1)
                both = jnp.dot(value, pair, preferred_element_type=F32)
                for i, part in ((1, both[:, width:]), (0, both[:, :width])):
                    message = (acc[t, d + i] + part).astype(BF16)
                    if d + i:
                        btx[t, d + i] = message
                        remote(
                            btx.at[t, d + i],
                            brx.at[t, d + i],
                            b_send.at[t],
                            b_recv.at[t],
                            (lanes[d + i], k),
                        ).start()
                    else:
                        own = message.astype(F32)
            sol_lv[level] = jnp.dot(
                value, inv_v[slot[level], 0], preferred_element_type=F32
            ).astype(BF16)
            if level == last:
                for r in range(rows):
                    half_out[r, 0] = half_lv[own_level[r]]
                out_copy(0, half_out).start()
            if t > 0:
                everything = near + far
                keys = []
                for w in everything:
                    for j in range(0, entries, 2):
                        pair = jnp.concatenate(
                            [picked(level, w, i, pl.ds(0, width)) for i in (j, j + 1)], axis=1
                        )
                        both = jnp.dot(value, pair, preferred_element_type=F32)
                        terms[w * entries + j] = both[:, :width]
                        terms[w * entries + j + 1] = both[:, width:]
                        for i in (j, j + 1):
                            keys.append(jnp.where(live[level], code_s[w, slot[level], i], -1))

                def later(target, carry):
                    for d in range(n_chain):
                        place = target * n_chain + lanes[d]
                        parts = [acc[target, d]] + [
                            jnp.where(key == place, terms[j], 0.0) for j, key in enumerate(keys)
                        ]
                        acc[target, d] = tree(parts)
                    return carry

                lax.fori_loop(0, t, later, 0)
                if not is_whole(t):
                    for row in candidates(t):
                        if row not in arrived:
                            arrived.add(row)
                            for which in far:
                                remote(
                                    blocks.at[which, row],
                                    blocks.at[which, row],
                                    x_send.at[which, row],
                                    x_recv.at[which, row],
                                    sibling,
                                ).wait_recv()
                    build(t, far, True)
            drain(brx.at[t], 1, n_chain - 1, b_recv.at[t])
            parts = [own] + [brx[t, d].astype(F32) for d in range(1, n_chain)]
            value = (half_lv[t].astype(F32) - tree(parts)).astype(BF16)

        sol_lv[0] = jnp.dot(value, inv_v[slot[0], 0], preferred_element_type=F32).astype(BF16)
        for r in range(rows):
            solved_out[r, 0] = sol_lv[own_level[r]]
        out_copy(1, solved_out).start()
        for level in range(last):
            drain(frx.at[level], 1, copies(level), f_send.at[level])
            drain(brx.at[level], 1, n_chain - 1, b_send.at[level])
        for row in range(rows):
            to_helper(row).wait_send()
        for copy in pats:
            copy.wait_send()
        out_copy(0, half_out).wait_send()
        out_copy(1, solved_out).wait_send()


def per_device(n_chain, n_col, rhs, pattern, factor, inverse, level_size):
    rows, _, probes, width = rhs.shape
    entries = factor.shape[2]
    levels = level_size.shape[0]
    workers = n_chain * (n_col // 2)
    dma = pltpu.SemaphoreType.DMA
    vmem = pl.BlockSpec(memory_space=pltpu.VMEM)
    hbm = pl.BlockSpec(memory_space=pl.ANY)
    out = pltpu.VMEM(rhs.shape, rhs.dtype)
    return pl.pallas_call(
        functools.partial(kernel, n_chain, n_col, levels),
        out_shape=(out, out),
        in_specs=[hbm, hbm, hbm, hbm, pl.BlockSpec(memory_space=pltpu.SMEM)],
        out_specs=(vmem, vmem),
        scratch_shapes=[
            pltpu.VMEM(rhs.shape, BF16),
            pltpu.VMEM(inverse.shape, BF16),
            pltpu.VMEM(factor.shape, BF16),
            pltpu.VMEM((n_col, rows, 1, entries), jnp.int32),
            pltpu.SMEM((n_col, rows, 1, entries), jnp.int32),
            pltpu.SMEM((n_col, rows, entries), jnp.int32),
            pltpu.VMEM((n_col, rows, entries, width, width), BF16),
            pltpu.VMEM((levels - 1, n_chain, width, width), BF16),
            pltpu.VMEM((n_chain * width, width), BF16),
            pltpu.VMEM((rows, probes, width), F32),
            pltpu.VMEM((levels * n_chain, probes, width), BF16),
            pltpu.VMEM((levels, workers, probes, width), BF16),
            pltpu.VMEM((levels, n_chain, probes, width), BF16),
            pltpu.VMEM((levels, n_chain, probes, width), BF16),
            pltpu.VMEM((levels, n_chain, probes, width), F32),
            pltpu.VMEM((n_col * entries, probes, width), F32),
            pltpu.VMEM((levels, probes, width), BF16),
            pltpu.VMEM((levels, probes, width), BF16),
            dma((3,)),
            dma((n_col,)),
            dma((levels,)),
            dma((levels,)),
            dma((levels,)),
            dma((levels,)),
            dma((n_col,)),
            dma((n_col,)),
            dma((rows,)),
            dma((rows,)),
            dma((rows,)),
            dma((rows,)),
            dma((n_col, rows)),
            dma((n_col, rows)),
            dma((2,)),
            dma((2,)),
        ],
        compiler_params=pltpu.CompilerParams(
            collective_id=0, has_side_effects=True, vmem_limit_bytes=56 * 1024 * 1024
        ),
    )(rhs, pattern, factor, inverse, level_size)


def solution(mesh):
    return jax.shard_map(
        functools.partial(per_device, mesh.shape["chain"], mesh.shape["col"]),
        mesh=mesh,
        in_specs=(
            P(None, "chain", None, None),
            P(None, "chain", "col"),
            P(None, "chain", "col", None, None),
            P(None, "chain", None, None),
            P(),
        ),
        out_specs=(P(None, "chain", None, None), P(None, "chain", None, None)),
        check_vma=False,
    )
```

```python
import functools

import jax
import jax.numpy as jnp
from jax import lax
from jax.experimental import pallas as pl
from jax.experimental.pallas import tpu as pltpu
from jax.sharding import PartitionSpec as P

MESH = pl.DeviceIdType.MESH
F32 = jnp.float32
BF16 = jnp.bfloat16
STEP = 16


def loop(count, body):
    if count <= 8:
        for i in range(count):
            body(i)
    else:
        lax.fori_loop(0, count, lambda i, carry: (body(i), carry)[1], 0)


def tree(parts):
    while len(parts) > 1:
        parts = [a + b for a, b in zip(parts[::2], parts[1::2])] + parts[len(parts) & ~1 :]
    return parts[0]


def kernel(
    n_chain,
    n_col,
    levels,
    rhs_hbm,
    pat_hbm,
    fac_hbm,
    inv_hbm,
    size_hbm,
    outs,
    rhs_v,
    inv_v,
    fac_v,
    pat_v,
    pat_s,
    code_s,
    blocks,
    dense,
    dense_t,
    base,
    store,
    frx,
    btx,
    brx,
    acc,
    terms,
    half_lv,
    sol_lv,
    size_ref,
    in_sem,
    pat_sem,
    f_send,
    f_recv,
    b_send,
    b_recv,
    p_send,
    p_recv,
    s_send,
    s_recv,
    w_send,
    w_recv,
    x_send,
    x_recv,
    o_send,
    o_recv,
):
    rows = rhs_v.shape[0]
    width = rhs_v.shape[3]
    entries = fac_v.shape[2]
    groups = n_col // 2
    last = levels - 1
    first_full = levels - 2
    me = lax.axis_index("chain")
    k = lax.axis_index("col")
    group = lax.div(k, 2)
    is_worker = lax.rem(k, 2) == 1
    sibling = (me, k + 1 - 2 * lax.rem(k, 2))

    load_rhs = pltpu.make_async_copy(rhs_hbm, rhs_v, in_sem.at[0])
    load_inv = pltpu.make_async_copy(inv_hbm, inv_v, in_sem.at[1])
    load_fac = pltpu.make_async_copy(fac_hbm, fac_v, in_sem.at[2])
    load_size = pltpu.make_async_copy(size_hbm, size_ref, in_sem.at[3])

    def start_loads():
        load_rhs.start()
        load_inv.start()
        load_size.start()
        load_fac.start()

    barrier = pltpu.get_barrier_semaphore()

    def flip(mask):
        out = me
        bit = 1
        while bit < n_chain:
            if mask & bit:
                out = out + bit - 2 * bit * lax.rem(lax.div(me, bit), 2)
            bit *= 2
        return out

    lanes = [flip(mask) for mask in range(n_chain)]
    columns = [2 * lax.rem(group + g, groups) + 1 for g in range(groups)]
    chain_order = sorted(range(1, n_chain), key=lambda d: -((d >> 1) + (d & 1)))
    peers = sorted(
        [(d, g) for d in range(n_chain) for g in range(groups) if d or g],
        key=lambda p: -((p[0] >> 1) + (p[0] & 1) + p[1]),
    )

    def remote(source, target, send_sem, recv_sem, device):
        return pltpu.make_async_remote_copy(
            src_ref=source,
            dst_ref=target,
            send_sem=send_sem,
            recv_sem=recv_sem,
            device_id=device,
            device_id_type=MESH,
        )

    def to_group(g):
        return (me, columns[g])

    def pat_to(which, device):
        return remote(pat_hbm, pat_v.at[which], p_send.at[which], p_recv.at[which], device)

    def to_sibling(row):
        return remote(
            blocks.at[0, row], blocks.at[1, row], s_send.at[row], s_recv.at[row], sibling
        )

    def to_helper(row):
        return remote(
            blocks.at[0, row], blocks.at[1, row], w_send.at[row], w_recv.at[row], sibling
        )

    def across(g, own, row):
        which = 2 * g + (0 if own == 1 else 1)
        return remote(
            blocks.at[own, row],
            blocks.at[which, row],
            x_send.at[which, row],
            x_recv.at[which, row],
            to_group(g),
        )

    def out_copy(i, ref):
        return remote(ref, ref, o_send.at[i], o_recv.at[i], sibling)

    def fold(row):
        for j in range(0, entries):
            block = jnp.dot(inv_v[row, 0], fac_v[row, 0, j], preferred_element_type=F32)
            blocks[0, row, j] = block.astype(BF16)

    @pl.when(jnp.logical_not(is_worker))
    def _():
        pl.semaphore_signal(barrier, inc=1, device_id=sibling, device_id_type=MESH)
        start_loads()
        load_size.wait()
        load_rhs.wait()
        load_inv.wait()
        load_fac.wait()
        fold(0)
        pl.semaphore_wait(barrier, groups)
        pats = [pat_to(1, sibling)] + [pat_to(2 * g + 1, to_group(g)) for g in range(1, groups)]
        for copy in pats:
            copy.start()
        to_sibling(0).start()
        for row in range(1, rows):
            fold(row)
            to_sibling(row).start()
        order = list(reversed(range(rows)))
        half = (rows + 1) // 2
        for part in (order[:half], order[half:]):
            for row in part:
                for g in range(1, groups):
                    across(g, 0, row).start()
            for row in part:
                to_helper(row).wait_recv()
                for g in range(1, groups):
                    across(g, 1, row).start()
        for copy in pats:
            copy.wait_send()
        for row in range(rows):
            to_sibling(row).wait_send()
            for g in range(1, groups):
                across(g, 0, row).wait_send()
                across(g, 1, row).wait_send()
        out_copy(0, outs.at[0]).wait_recv()
        out_copy(1, outs.at[1]).wait_recv()

    @pl.when(is_worker)
    def _():
        for d, g in peers:
            pl.semaphore_signal(
                barrier, inc=1, device_id=(lanes[d], columns[g]), device_id_type=MESH
            )
        for g in range(groups):
            pl.semaphore_signal(
                barrier, inc=1, device_id=(me, columns[g] - 1), device_id_type=MESH
            )
        start_loads()
        own_pat = pltpu.make_async_copy(pat_hbm, pat_s.at[0], pat_sem.at[0])
        own_pat.start()

        load_rhs.wait()
        load_inv.wait()

        def times_inverse_t(row):
            return lax.dot_general(
                rhs_v[row, 0], inv_v[row, 0], (((1,), (1,)), ((), ())), preferred_element_type=F32
            )

        first = times_inverse_t(0)
        frx[0, 0] = first.astype(BF16)
        pl.semaphore_wait(barrier, n_chain * groups)

        def drain(ref, start, count, sem):
            part = ref.at[pl.ds(start, count)]
            pltpu.make_async_copy(part, part, sem).wait()

        def share(level, whole):
            for d, g in [(d, 0) for d in chain_order] if whole else peers:
                remote(
                    frx.at[level, 0],
                    frx.at[level, g * n_chain + d],
                    f_send.at[level],
                    f_recv.at[level],
                    (lanes[d], columns[g]),
                ).start()

        def is_whole(level):
            return level == 0 or level >= first_full

        def copies(level):
            return (n_chain if is_whole(level) else n_chain * groups) - 1

        def candidates(level):
            return list(range(max(0, rows - levels + level), min(level, rows - 1) + 1))

        def picked(level, which, j, at):
            first_row, *others = candidates(level)
            block = blocks[which, first_row, j, at, :]
            for row in others:
                block = jnp.where(slot[level] == row, blocks[which, row, j, at, :], block)
            return block

        def fill_codes(whiches):
            for which in whiches:
                for row in range(rows):
                    for j in range(entries):
                        target = pat_s[which, row, 0, j]
                        code_s[which, row, j] = level_of(target) * n_chain + lax.rem(
                            target, n_chain
                        )

        def build(level, whiches, add):
            keys = [
                jnp.where(live[level], code_s[w, slot[level], j], -1) - (level - 1) * n_chain
                for w in whiches
                for j in range(entries)
            ]

            def chunk(i, carry):
                at = pl.ds(pl.multiple_of(i * STEP, STEP), STEP)
                found = [picked(level, w, j, at) for w in whiches for j in range(entries)]
                for d in range(n_chain):
                    parts = [
                        jnp.where(key == lanes[d], block, jnp.zeros_like(block))
                        for key, block in zip(keys, found)
                    ]
                    if add:
                        parts.append(dense[level - 1, d, at, :])
                    dense[level - 1, d, at, :] = tree(parts)
                return carry

            lax.fori_loop(0, width // STEP, chunk, 0)

        def turn(level):
            def one(d):
                at = pl.ds(d * width, width)
                dense_t[at, :] = dense[level - 1, d].astype(F32).T.astype(BF16)

            loop(n_chain, one)

        def older(level, whiches):
            sums = None
            for w in whiches:
                for j in range(0, entries, 2):
                    pair = range(j, min(j + 2, entries))
                    left = jnp.concatenate([store[code_s[w, slot[level], i]] for i in pair], axis=1)
                    right = jnp.concatenate(
                        [picked(level, w, i, pl.ds(0, width)) for i in pair], axis=1
                    )
                    term = lax.dot_general(
                        left, right, (((1,), (1,)), ((), ())), preferred_element_type=F32
                    )
                    sums = term if sums is None else sums + term
            return sums

        near = [0, 1]
        far = list(range(2, n_col))
        share(0, True)

        load_size.wait()
        ends = []
        running = jnp.int32(0)
        for level in range(levels):
            running = running + size_ref[level]
            ends.append(running)

        def level_of(position):
            found = jnp.int32(0)
            for end in ends[:-1]:
                found = found + (position >= end).astype(jnp.int32)
            return found

        own_level = [level_of(row * n_chain + me) for row in range(rows)]
        slot = []
        live = []
        for level in range(levels):
            here = jnp.int32(0)
            count = jnp.int32(0)
            for row in range(rows):
                match = own_level[row] == level
                here = jnp.where(match, row, here)
                count = count + match.astype(jnp.int32)
            slot.append(here)
            live.append(count > 0)

        load_fac.wait()
        for row in reversed(range(rows)):
            fold(row)
            to_helper(row).start()
        pats = [pat_to(2 * g, to_group(g)) for g in range(1, groups)]
        for copy in pats:
            copy.start()
        base[0] = first
        for row in range(1, rows):
            base[row] = times_inverse_t(row)
        store[...] = jnp.zeros_like(store)
        acc[...] = jnp.zeros_like(acc)
        own_pat.wait()
        pat_to(1, sibling).wait_recv()
        other_pat = pltpu.make_async_copy(pat_v.at[1], pat_s.at[1], pat_sem.at[1])
        other_pat.start()
        other_pat.wait()
        fill_codes(near)
        for row in range(rows):
            to_sibling(row).wait_recv()
        build(1, near, False)
        turn(1)

        keep = (group == 0).astype(F32)
        for level in range(1, levels):
            whole = is_whole(level)
            before = base[slot[level]]
            if not whole:
                before = before * keep
            if level > 1:
                before = before - older(level, near + far if whole else near)
            drain(frx.at[level - 1], 1, copies(level - 1), f_recv.at[level - 1])
            found = []
            for d in range(n_chain):
                if is_whole(level - 1):
                    found.append(frx[level - 1, d])
                else:
                    parts = [frx[level - 1, g * n_chain + d].astype(F32) for g in range(groups)]
                    found.append(tree(parts).astype(BF16))
            sums = jnp.dot(
                jnp.concatenate(found, axis=1), dense_t[...], preferred_element_type=F32
            )
            value = (before - sums).astype(BF16)
            half_lv[level - 1] = found[0]
            if level == last:
                half_lv[level] = value
                break
            frx[level, 0] = value
            share(level, whole)
            for d in range(n_chain):
                store[(level - 1) * n_chain + lanes[d]] = found[d]
            if level + 1 == first_full:
                moved = []
                for which in far:
                    pat_to(which, sibling).wait_recv()
                    moved.append(
                        pltpu.make_async_copy(pat_v.at[which], pat_s.at[which], pat_sem.at[which])
                    )
                    moved[-1].start()
                for copy in moved:
                    copy.wait()
                fill_codes(far)
            if is_whole(level + 1):
                for which in far:
                    for row in candidates(level + 1):
                        if level + 1 == first_full:
                            remote(
                                blocks.at[which, row],
                                blocks.at[which, row],
                                x_send.at[which, row],
                                x_recv.at[which, row],
                                sibling,
                            ).wait_recv()
            build(level + 1, near + far if is_whole(level + 1) else near, False)
            turn(level + 1)

        arrived = set(candidates(first_full)) | set(candidates(last))
        for level in reversed(range(1, levels)):
            t = level - 1
            for d in reversed(range(0, n_chain, 2)):
                pair = jnp.concatenate([dense[t, d], dense[t, d + 1]], axis=1)
                both = jnp.dot(value, pair, preferred_element_type=F32)
                for i, part in ((1, both[:, width:]), (0, both[:, :width])):
                    message = (acc[t, d + i] + part).astype(BF16)
                    if d + i:
                        btx[t, d + i] = message
                        remote(
                            btx.at[t, d + i],
                            brx.at[t, d + i],
                            b_send.at[t],
                            b_recv.at[t],
                            (lanes[d + i], k),
                        ).start()
                    else:
                        own = message.astype(F32)
            sol_lv[level] = jnp.dot(
                value, inv_v[slot[level], 0], preferred_element_type=F32
            ).astype(BF16)
            if level == last:
                for r in range(rows):
                    outs[0, r, 0] = half_lv[own_level[r]]
                out_copy(0, outs.at[0]).start()
            if t > 0:
                everything = near + far
                keys = []
                for w in everything:
                    for j in range(0, entries, 2):
                        pair = jnp.concatenate(
                            [picked(level, w, i, pl.ds(0, width)) for i in (j, j + 1)], axis=1
                        )
                        both = jnp.dot(value, pair, preferred_element_type=F32)
                        terms[w * entries + j] = both[:, :width]
                        terms[w * entries + j + 1] = both[:, width:]
                        for i in (j, j + 1):
                            keys.append(jnp.where(live[level], code_s[w, slot[level], i], -1))

                def later(target, carry):
                    for d in range(n_chain):
                        place = target * n_chain + lanes[d]
                        parts = [acc[target, d]] + [
                            jnp.where(key == place, terms[j], 0.0) for j, key in enumerate(keys)
                        ]
                        acc[target, d] = tree(parts)
                    return carry

                lax.fori_loop(0, t, later, 0)
                if not is_whole(t):
                    for row in candidates(t):
                        if row not in arrived:
                            arrived.add(row)
                            for which in far:
                                remote(
                                    blocks.at[which, row],
                                    blocks.at[which, row],
                                    x_send.at[which, row],
                                    x_recv.at[which, row],
                                    sibling,
                                ).wait_recv()
                    build(t, far, True)
            drain(brx.at[t], 1, n_chain - 1, b_recv.at[t])
            parts = [own] + [brx[t, d].astype(F32) for d in range(1, n_chain)]
            value = (half_lv[t].astype(F32) - tree(parts)).astype(BF16)

        sol_lv[0] = jnp.dot(value, inv_v[slot[0], 0], preferred_element_type=F32).astype(BF16)
        for r in range(rows):
            outs[1, r, 0] = sol_lv[own_level[r]]
        out_copy(1, outs.at[1]).start()
        for level in range(last):
            drain(frx.at[level], 1, copies(level), f_send.at[level])
            drain(brx.at[level], 1, n_chain - 1, b_send.at[level])
        for row in range(rows):
            to_helper(row).wait_send()
        for copy in pats:
            copy.wait_send()
        out_copy(0, outs.at[0]).wait_send()
        out_copy(1, outs.at[1]).wait_send()


def per_device(n_chain, n_col, rhs, pattern, factor, inverse, level_size):
    rows, _, probes, width = rhs.shape
    entries = factor.shape[2]
    levels = level_size.shape[0]
    workers = n_chain * (n_col // 2)
    dma = pltpu.SemaphoreType.DMA
    vmem = pl.BlockSpec(memory_space=pltpu.VMEM)
    hbm = pl.BlockSpec(memory_space=pl.ANY)
    out = pltpu.VMEM((2,) + rhs.shape, rhs.dtype)
    both = pl.pallas_call(
        functools.partial(kernel, n_chain, n_col, levels),
        out_shape=out,
        in_specs=[hbm, hbm, hbm, hbm, hbm],
        out_specs=vmem,
        scratch_shapes=[
            pltpu.VMEM(rhs.shape, BF16),
            pltpu.VMEM(inverse.shape, BF16),
            pltpu.VMEM(factor.shape, BF16),
            pltpu.VMEM((n_col, rows, 1, entries), jnp.int32),
            pltpu.SMEM((n_col, rows, 1, entries), jnp.int32),
            pltpu.SMEM((n_col, rows, entries), jnp.int32),
            pltpu.VMEM((n_col, rows, entries, width, width), BF16),
            pltpu.VMEM((levels - 1, n_chain, width, width), BF16),
            pltpu.VMEM((n_chain * width, width), BF16),
            pltpu.VMEM((rows, probes, width), F32),
            pltpu.VMEM((levels * n_chain, probes, width), BF16),
            pltpu.VMEM((levels, workers, probes, width), BF16),
            pltpu.VMEM((levels, n_chain, probes, width), BF16),
            pltpu.VMEM((levels, n_chain, probes, width), BF16),
            pltpu.VMEM((levels, n_chain, probes, width), F32),
            pltpu.VMEM((n_col * entries, probes, width), F32),
            pltpu.VMEM((levels, probes, width), BF16),
            pltpu.VMEM((levels, probes, width), BF16),
            pltpu.SMEM((levels,), jnp.int32),
            dma((4,)),
            dma((n_col,)),
            dma((levels,)),
            dma((levels,)),
            dma((levels,)),
            dma((levels,)),
            dma((n_col,)),
            dma((n_col,)),
            dma((rows,)),
            dma((rows,)),
            dma((rows,)),
            dma((rows,)),
            dma((n_col, rows)),
            dma((n_col, rows)),
            dma((2,)),
            dma((2,)),
        ],
        compiler_params=pltpu.CompilerParams(
            collective_id=0, has_side_effects=True, vmem_limit_bytes=56 * 1024 * 1024
        ),
    )(rhs, pattern, factor, inverse, level_size)
    return both[0], both[1]


def solution(mesh):
    return jax.shard_map(
        functools.partial(per_device, mesh.shape["chain"], mesh.shape["col"]),
        mesh=mesh,
        in_specs=(
            P(None, "chain", None, None),
            P(None, "chain", "col"),
            P(None, "chain", "col", None, None),
            P(None, "chain", None, None),
            P(),
        ),
        out_specs=(P(None, "chain", None, None), P(None, "chain", None, None)),
        check_vma=False,
    )
```

```python
import functools

import jax
import jax.numpy as jnp
from jax import lax
from jax.experimental import pallas as pl
from jax.experimental.pallas import tpu as pltpu
from jax.sharding import PartitionSpec as P

MESH = pl.DeviceIdType.MESH
F32 = jnp.float32
BF16 = jnp.bfloat16
STEP = 16


def loop(count, body):
    if count <= 8:
        for i in range(count):
            body(i)
    else:
        lax.fori_loop(0, count, lambda i, carry: (body(i), carry)[1], 0)


def tree(parts):
    while len(parts) > 1:
        parts = [a + b for a, b in zip(parts[::2], parts[1::2])] + parts[len(parts) & ~1 :]
    return parts[0]


def kernel(
    n_chain,
    n_col,
    levels,
    rhs_hbm,
    pat_hbm,
    fac_hbm,
    inv_hbm,
    size_hbm,
    outs,
    rhs_v,
    inv_v,
    fac_v,
    pat_v,
    pat_s,
    code_s,
    blocks,
    dense,
    dense_t,
    base,
    store,
    frx,
    btx,
    brx,
    acc,
    terms,
    half_lv,
    sol_lv,
    size_ref,
    in_sem,
    pat_sem,
    f_send,
    f_recv,
    b_send,
    b_recv,
    p_send,
    p_recv,
    s_send,
    s_recv,
    w_send,
    w_recv,
    x_send,
    x_recv,
    o_send,
    o_recv,
    v_send,
    v_recv,
    h_send,
    h_recv,
    ready,
):
    rows = rhs_v.shape[0]
    width = rhs_v.shape[3]
    entries = fac_v.shape[2]
    groups = n_col // 2
    last = levels - 1
    first_full = levels - 2
    me = lax.axis_index("chain")
    k = lax.axis_index("col")
    group = lax.div(k, 2)
    is_worker = lax.rem(k, 2) == 1
    sibling = (me, k + 1 - 2 * lax.rem(k, 2))

    load_rhs = pltpu.make_async_copy(rhs_hbm, rhs_v, in_sem.at[0])
    load_inv = pltpu.make_async_copy(inv_hbm, inv_v, in_sem.at[1])
    load_fac = pltpu.make_async_copy(fac_hbm, fac_v, in_sem.at[2])
    load_size = pltpu.make_async_copy(size_hbm, size_ref, in_sem.at[3])

    def start_loads():
        load_rhs.start()
        load_inv.start()
        load_size.start()
        load_fac.start()

    barrier = pltpu.get_barrier_semaphore()

    def flip(mask):
        out = me
        bit = 1
        while bit < n_chain:
            if mask & bit:
                out = out + bit - 2 * bit * lax.rem(lax.div(me, bit), 2)
            bit *= 2
        return out

    lanes = [flip(mask) for mask in range(n_chain)]
    columns = [2 * lax.rem(group + g, groups) + 1 for g in range(groups)]
    chain_order = sorted(range(1, n_chain), key=lambda d: -((d >> 1) + (d & 1)))
    peers = sorted(
        [(d, g) for d in range(n_chain) for g in range(groups) if d or g],
        key=lambda p: -((p[0] >> 1) + (p[0] & 1) + p[1]),
    )

    def remote(source, target, send_sem, recv_sem, device):
        return pltpu.make_async_remote_copy(
            src_ref=source,
            dst_ref=target,
            send_sem=send_sem,
            recv_sem=recv_sem,
            device_id=device,
            device_id_type=MESH,
        )

    def to_group(g):
        return (me, columns[g])

    def pat_to(which, device):
        return remote(pat_hbm, pat_v.at[which], p_send.at[which], p_recv.at[which], device)

    def to_sibling(row):
        return remote(
            blocks.at[0, row], blocks.at[1, row], s_send.at[row], s_recv.at[row], sibling
        )

    def to_helper(row):
        return remote(
            blocks.at[0, row], blocks.at[1, row], w_send.at[row], w_recv.at[row], sibling
        )

    def across(g, own, row):
        which = 2 * g + (0 if own == 1 else 1)
        return remote(
            blocks.at[own, row],
            blocks.at[which, row],
            x_send.at[which, row],
            x_recv.at[which, row],
            to_group(g),
        )

    half_copy = remote(outs.at[0], outs.at[0], o_send, o_recv, sibling)

    def fold(row):
        for j in range(0, entries):
            block = jnp.dot(inv_v[row, 0], fac_v[row, 0, j], preferred_element_type=F32)
            blocks[0, row, j] = block.astype(BF16)

    def plan():
        load_size.wait()
        ends = []
        running = jnp.int32(0)
        for level in range(levels):
            running = running + size_ref[level]
            ends.append(running)

        def level_of(position):
            found = jnp.int32(0)
            for end in ends[:-1]:
                found = found + (position >= end).astype(jnp.int32)
            return found

        return level_of, [level_of(row * n_chain + me) for row in range(rows)]

    def times_inverse_t(row):
        return lax.dot_general(
            rhs_v[row, 0], inv_v[row, 0], (((1,), (1,)), ((), ())), preferred_element_type=F32
        )

    def drain(ref, start, count, sem):
        part = ref.at[pl.ds(start, count)]
        pltpu.make_async_copy(part, part, sem).wait()

    def less(half, parts):
        return (half.astype(F32) - tree([part.astype(F32) for part in parts])).astype(BF16)

    def times_inverse(value, row):
        return jnp.dot(value, inv_v[row, 0], preferred_element_type=F32).astype(BF16)

    later_levels = pl.ds(1, levels - 1)
    solved_copy = remote(
        sol_lv.at[later_levels], sol_lv.at[later_levels], v_send, v_recv, sibling
    )

    @pl.when(jnp.logical_not(is_worker))
    def _():
        pl.semaphore_signal(barrier, inc=1, device_id=sibling, device_id_type=MESH)
        start_loads()
        load_rhs.wait()
        load_inv.wait()
        load_fac.wait()
        fold(0)
        pl.semaphore_wait(barrier, groups)
        pats = [pat_to(1, sibling)] + [pat_to(2 * g + 1, to_group(g)) for g in range(1, groups)]
        for copy in pats:
            copy.start()
        to_sibling(0).start()
        for row in range(1, rows):
            fold(row)
            to_sibling(row).start()
        order = list(reversed(range(rows)))
        half = (rows + 1) // 2
        for part in (order[:half], order[half:]):
            for row in part:
                for g in range(1, groups):
                    across(g, 0, row).start()
            for row in part:
                to_helper(row).wait_recv()
                for g in range(1, groups):
                    across(g, 1, row).start()
        for copy in pats:
            copy.wait_send()
        for row in range(rows):
            to_sibling(row).wait_send()
            for g in range(1, groups):
                across(g, 0, row).wait_send()
                across(g, 1, row).wait_send()
        own_level = plan()[1]
        half = times_inverse_t(0).astype(BF16)
        half_copy.wait_recv()
        solved_copy.wait_recv()
        drain(brx.at[0], 0, n_chain, h_recv)
        value = less(half, [brx[0, d] for d in range(n_chain)])
        sol_lv[0] = times_inverse(value, 0)
        for r in range(rows):
            outs[1, r, 0] = sol_lv[own_level[r]]

    @pl.when(is_worker)
    def _():
        for d in chain_order:
            pl.semaphore_signal(barrier, inc=1, device_id=(lanes[d], k), device_id_type=MESH)
        for g in range(groups):
            if g:
                pl.semaphore_signal(barrier, inc=1, device_id=to_group(g), device_id_type=MESH)
            pl.semaphore_signal(
                barrier, inc=1, device_id=(me, columns[g] - 1), device_id_type=MESH
            )
        start_loads()
        own_pat = pltpu.make_async_copy(pat_hbm, pat_s.at[0], pat_sem.at[0])
        own_pat.start()

        load_rhs.wait()
        load_inv.wait()

        first = times_inverse_t(0)
        frx[0, 0] = first.astype(BF16)
        pl.semaphore_wait(barrier, n_chain + groups - 1)

        def share(level, whole):
            for d, g in [(d, 0) for d in chain_order] if whole else peers:
                remote(
                    frx.at[level, 0],
                    frx.at[level, g * n_chain + d],
                    f_send.at[level],
                    f_recv.at[level],
                    (lanes[d], columns[g]),
                ).start()

        def is_whole(level):
            return level == 0 or level >= first_full

        def copies(level):
            return (n_chain if is_whole(level) else n_chain * groups) - 1

        def candidates(level):
            return list(range(max(0, rows - levels + level), min(level, rows - 1) + 1))

        def picked(level, which, j, at):
            first_row, *others = candidates(level)
            block = blocks[which, first_row, j, at, :]
            for row in others:
                block = jnp.where(slot[level] == row, blocks[which, row, j, at, :], block)
            return block

        def fill_codes(whiches):
            for which in whiches:
                for row in range(rows):
                    for j in range(entries):
                        target = pat_s[which, row, 0, j]
                        code_s[which, row, j] = level_of(target) * n_chain + lax.rem(
                            target, n_chain
                        )

        def build(level, whiches, add):
            keys = [
                jnp.where(live[level], code_s[w, slot[level], j], -1) - (level - 1) * n_chain
                for w in whiches
                for j in range(entries)
            ]

            def chunk(i, carry):
                at = pl.ds(pl.multiple_of(i * STEP, STEP), STEP)
                found = [picked(level, w, j, at) for w in whiches for j in range(entries)]
                for d in range(n_chain):
                    parts = [
                        jnp.where(key == lanes[d], block, jnp.zeros_like(block))
                        for key, block in zip(keys, found)
                    ]
                    if add:
                        parts.append(dense[level - 1, d, at, :])
                    dense[level - 1, d, at, :] = tree(parts)
                return carry

            lax.fori_loop(0, width // STEP, chunk, 0)

        def turn(level):
            def one(d):
                at = pl.ds(d * width, width)
                dense_t[at, :] = dense[level - 1, d].astype(F32).T.astype(BF16)

            loop(n_chain, one)

        def older(level, whiches):
            sums = None
            for w in whiches:
                for j in range(0, entries, 2):
                    pair = range(j, min(j + 2, entries))
                    left = jnp.concatenate([store[code_s[w, slot[level], i]] for i in pair], axis=1)
                    right = jnp.concatenate(
                        [picked(level, w, i, pl.ds(0, width)) for i in pair], axis=1
                    )
                    term = lax.dot_general(
                        left, right, (((1,), (1,)), ((), ())), preferred_element_type=F32
                    )
                    sums = term if sums is None else sums + term
            return sums

        near = [0, 1]
        far = list(range(2, n_col))
        share(0, True)
        for g in range(1, groups):
            pl.semaphore_signal(ready, inc=1, device_id=to_group(g), device_id_type=MESH)

        level_of, own_level = plan()
        slot = []
        live = []
        for level in range(levels):
            here = jnp.int32(0)
            count = jnp.int32(0)
            for row in range(rows):
                match = own_level[row] == level
                here = jnp.where(match, row, here)
                count = count + match.astype(jnp.int32)
            slot.append(here)
            live.append(count > 0)

        load_fac.wait()
        for row in reversed(range(rows)):
            fold(row)
            to_helper(row).start()
        pats = [pat_to(2 * g, to_group(g)) for g in range(1, groups)]
        for copy in pats:
            copy.start()
        base[0] = first
        for row in range(1, rows):
            base[row] = times_inverse_t(row)
        store[...] = jnp.zeros_like(store)
        acc[...] = jnp.zeros_like(acc)
        own_pat.wait()
        pat_to(1, sibling).wait_recv()
        other_pat = pltpu.make_async_copy(pat_v.at[1], pat_s.at[1], pat_sem.at[1])
        other_pat.start()
        other_pat.wait()
        fill_codes(near)
        for row in range(rows):
            to_sibling(row).wait_recv()
        build(1, near, False)
        turn(1)
        if groups > 1:
            pl.semaphore_wait(ready, groups - 1)

        keep = (group == 0).astype(F32)
        for level in range(1, levels):
            whole = is_whole(level)
            before = base[slot[level]]
            if not whole:
                before = before * keep
            if level > 1:
                before = before - older(level, near + far if whole else near)
            drain(frx.at[level - 1], 1, copies(level - 1), f_recv.at[level - 1])
            found = []
            for d in range(n_chain):
                if is_whole(level - 1):
                    found.append(frx[level - 1, d])
                else:
                    parts = [frx[level - 1, g * n_chain + d].astype(F32) for g in range(groups)]
                    found.append(tree(parts).astype(BF16))
            sums = jnp.dot(
                jnp.concatenate(found, axis=1), dense_t[...], preferred_element_type=F32
            )
            value = (before - sums).astype(BF16)
            half_lv[level - 1] = found[0]
            if level == last:
                half_lv[level] = value
                break
            frx[level, 0] = value
            share(level, whole)
            for d in range(n_chain):
                store[(level - 1) * n_chain + lanes[d]] = found[d]
            if level + 1 == first_full:
                moved = []
                for which in far:
                    pat_to(which, sibling).wait_recv()
                    moved.append(
                        pltpu.make_async_copy(pat_v.at[which], pat_s.at[which], pat_sem.at[which])
                    )
                    moved[-1].start()
                for copy in moved:
                    copy.wait()
                fill_codes(far)
            if is_whole(level + 1):
                for which in far:
                    for row in candidates(level + 1):
                        if level + 1 == first_full:
                            remote(
                                blocks.at[which, row],
                                blocks.at[which, row],
                                x_send.at[which, row],
                                x_recv.at[which, row],
                                sibling,
                            ).wait_recv()
            build(level + 1, near + far if is_whole(level + 1) else near, False)
            turn(level + 1)

        arrived = set(candidates(first_full)) | set(candidates(last))
        for level in reversed(range(1, levels)):
            t = level - 1
            for d in reversed(range(0, n_chain, 2)):
                pair = jnp.concatenate([dense[t, d], dense[t, d + 1]], axis=1)
                both = jnp.dot(value, pair, preferred_element_type=F32)
                for i, part in ((1, both[:, width:]), (0, both[:, :width])):
                    message = (acc[t, d + i] + part).astype(BF16)
                    if d + i or t == 0:
                        btx[t, d + i] = message
                    if t == 0:
                        remote(
                            btx.at[t, d + i],
                            brx.at[t, d + i],
                            h_send,
                            h_recv,
                            (lanes[d + i], k - 1),
                        ).start()
                    if d + i:
                        remote(
                            btx.at[t, d + i],
                            brx.at[t, d + i],
                            b_send.at[t],
                            b_recv.at[t],
                            (lanes[d + i], k),
                        ).start()
                    else:
                        own = message
            sol_lv[level] = times_inverse(value, slot[level])
            if t == 0:
                solved_copy.start()
            if level == last:
                for r in range(rows):
                    outs[0, r, 0] = half_lv[own_level[r]]
                half_copy.start()
            if t > 0:
                everything = near + far
                keys = []
                for w in everything:
                    for j in range(0, entries, 2):
                        pair = jnp.concatenate(
                            [picked(level, w, i, pl.ds(0, width)) for i in (j, j + 1)], axis=1
                        )
                        both = jnp.dot(value, pair, preferred_element_type=F32)
                        terms[w * entries + j] = both[:, :width]
                        terms[w * entries + j + 1] = both[:, width:]
                        for i in (j, j + 1):
                            keys.append(jnp.where(live[level], code_s[w, slot[level], i], -1))

                def later(target, carry):
                    for d in range(n_chain):
                        place = target * n_chain + lanes[d]
                        parts = [acc[target, d]] + [
                            jnp.where(key == place, terms[j], 0.0) for j, key in enumerate(keys)
                        ]
                        acc[target, d] = tree(parts)
                    return carry

                lax.fori_loop(0, t, later, 0)
                if not is_whole(t):
                    for row in candidates(t):
                        if row not in arrived:
                            arrived.add(row)
                            for which in far:
                                remote(
                                    blocks.at[which, row],
                                    blocks.at[which, row],
                                    x_send.at[which, row],
                                    x_recv.at[which, row],
                                    sibling,
                                ).wait_recv()
                    build(t, far, True)
            drain(brx.at[t], 1, n_chain - 1, b_recv.at[t])
            value = less(half_lv[t], [own] + [brx[t, d] for d in range(1, n_chain)])

        sol_lv[0] = times_inverse(value, 0)
        for r in range(rows):
            outs[1, r, 0] = sol_lv[own_level[r]]
        for level in range(last):
            drain(frx.at[level], 1, copies(level), f_send.at[level])
            drain(brx.at[level], 1, n_chain - 1, b_send.at[level])
        for row in range(rows):
            to_helper(row).wait_send()
        for copy in pats:
            copy.wait_send()
        half_copy.wait_send()
        solved_copy.wait_send()
        drain(btx.at[0], 0, n_chain, h_send)


def per_device(n_chain, n_col, rhs, pattern, factor, inverse, level_size):
    rows, _, probes, width = rhs.shape
    entries = factor.shape[2]
    levels = level_size.shape[0]
    workers = n_chain * (n_col // 2)
    dma = pltpu.SemaphoreType.DMA
    vmem = pl.BlockSpec(memory_space=pltpu.VMEM)
    hbm = pl.BlockSpec(memory_space=pl.ANY)
    out = pltpu.VMEM((2,) + rhs.shape, rhs.dtype)
    both = pl.pallas_call(
        functools.partial(kernel, n_chain, n_col, levels),
        out_shape=out,
        in_specs=[hbm, hbm, hbm, hbm, hbm],
        out_specs=vmem,
        scratch_shapes=[
            pltpu.VMEM(rhs.shape, BF16),
            pltpu.VMEM(inverse.shape, BF16),
            pltpu.VMEM(factor.shape, BF16),
            pltpu.VMEM((n_col, rows, 1, entries), jnp.int32),
            pltpu.SMEM((n_col, rows, 1, entries), jnp.int32),
            pltpu.SMEM((n_col, rows, entries), jnp.int32),
            pltpu.VMEM((n_col, rows, entries, width, width), BF16),
            pltpu.VMEM((levels - 1, n_chain, width, width), BF16),
            pltpu.VMEM((n_chain * width, width), BF16),
            pltpu.VMEM((rows, probes, width), F32),
            pltpu.VMEM((levels * n_chain, probes, width), BF16),
            pltpu.VMEM((levels, workers, probes, width), BF16),
            pltpu.VMEM((levels, n_chain, probes, width), BF16),
            pltpu.VMEM((levels, n_chain, probes, width), BF16),
            pltpu.VMEM((levels, n_chain, probes, width), F32),
            pltpu.VMEM((n_col * entries, probes, width), F32),
            pltpu.VMEM((levels, probes, width), BF16),
            pltpu.VMEM((levels, probes, width), BF16),
            pltpu.SMEM((levels,), jnp.int32),
            dma((4,)),
            dma((n_col,)),
            dma((levels,)),
            dma((levels,)),
            dma((levels,)),
            dma((levels,)),
            dma((n_col,)),
            dma((n_col,)),
            dma((rows,)),
            dma((rows,)),
            dma((rows,)),
            dma((rows,)),
            dma((n_col, rows)),
            dma((n_col, rows)),
            dma,
            dma,
            dma,
            dma,
            dma,
            dma,
            pltpu.SemaphoreType.REGULAR,
        ],
        compiler_params=pltpu.CompilerParams(
            collective_id=0, has_side_effects=True, vmem_limit_bytes=56 * 1024 * 1024
        ),
    )(rhs, pattern, factor, inverse, level_size)
    return both[0], both[1]


def solution(mesh):
    return jax.shard_map(
        functools.partial(per_device, mesh.shape["chain"], mesh.shape["col"]),
        mesh=mesh,
        in_specs=(
            P(None, "chain", None, None),
            P(None, "chain", "col"),
            P(None, "chain", "col", None, None),
            P(None, "chain", None, None),
            P(),
        ),
        out_specs=(P(None, "chain", None, None), P(None, "chain", None, None)),
        check_vma=False,
    )
```

```python
import functools

import jax
import jax.numpy as jnp
from jax import lax
from jax.experimental import pallas as pl
from jax.experimental.pallas import tpu as pltpu
from jax.sharding import PartitionSpec as P

MESH = pl.DeviceIdType.MESH
F32 = jnp.float32
BF16 = jnp.bfloat16
STEP = 16


def loop(count, body):
    if count <= 8:
        for i in range(count):
            body(i)
    else:
        lax.fori_loop(0, count, lambda i, carry: (body(i), carry)[1], 0)


def tree(parts):
    while len(parts) > 1:
        parts = [a + b for a, b in zip(parts[::2], parts[1::2])] + parts[len(parts) & ~1 :]
    return parts[0]


def kernel(
    n_chain,
    n_col,
    levels,
    rhs_hbm,
    pat_hbm,
    fac_hbm,
    inv_hbm,
    size_hbm,
    outs,
    rhs_v,
    inv_v,
    fac_v,
    pat_v,
    pat_s,
    code_s,
    blocks,
    dense,
    dense_t,
    base,
    store,
    frx,
    btx,
    brx,
    acc,
    terms,
    half_lv,
    sol_lv,
    size_ref,
    in_sem,
    pat_sem,
    f_send,
    f_recv,
    b_send,
    b_recv,
    p_send,
    p_recv,
    s_send,
    s_recv,
    w_send,
    w_recv,
    x_send,
    x_recv,
    o_send,
    o_recv,
    v_send,
    v_recv,
    h_send,
    h_recv,
    ready,
):
    rows = rhs_v.shape[0]
    width = rhs_v.shape[3]
    entries = fac_v.shape[2]
    groups = n_col // 2
    last = levels - 1
    first_full = levels - 2
    me = lax.axis_index("chain")
    k = lax.axis_index("col")
    group = lax.div(k, 2)
    is_worker = lax.rem(k, 2) == 1
    sibling = (me, k + 1 - 2 * lax.rem(k, 2))

    load_rhs = pltpu.make_async_copy(rhs_hbm, rhs_v, in_sem.at[0])
    load_inv = pltpu.make_async_copy(inv_hbm, inv_v, in_sem.at[1])
    load_fac = pltpu.make_async_copy(fac_hbm, fac_v, in_sem.at[2])
    load_size = pltpu.make_async_copy(size_hbm, size_ref, in_sem.at[3])

    def start_loads():
        load_rhs.start()
        load_inv.start()
        load_size.start()
        load_fac.start()

    barrier = pltpu.get_barrier_semaphore()

    def flip(mask):
        out = me
        bit = 1
        while bit < n_chain:
            if mask & bit:
                out = out + bit - 2 * bit * lax.rem(lax.div(me, bit), 2)
            bit *= 2
        return out

    lanes = [flip(mask) for mask in range(n_chain)]
    columns = [2 * lax.rem(group + g, groups) + 1 for g in range(groups)]
    chain_order = sorted(range(1, n_chain), key=lambda d: -((d >> 1) + (d & 1)))
    peers = sorted(
        [(d, g) for d in range(n_chain) for g in range(groups) if d or g],
        key=lambda p: -((p[0] >> 1) + (p[0] & 1) + p[1]),
    )

    def remote(source, target, send_sem, recv_sem, device):
        return pltpu.make_async_remote_copy(
            src_ref=source,
            dst_ref=target,
            send_sem=send_sem,
            recv_sem=recv_sem,
            device_id=device,
            device_id_type=MESH,
        )

    def to_group(g):
        return (me, columns[g])

    def pat_to(which, device):
        return remote(pat_hbm, pat_v.at[which], p_send.at[which], p_recv.at[which], device)

    def to_sibling(row):
        return remote(
            blocks.at[0, row], blocks.at[1, row], s_send.at[row], s_recv.at[row], sibling
        )

    def to_helper(row):
        return remote(
            blocks.at[0, row], blocks.at[1, row], w_send.at[row], w_recv.at[row], sibling
        )

    def across(g, own, row):
        which = 2 * g + (0 if own == 1 else 1)
        return remote(
            blocks.at[own, row],
            blocks.at[which, row],
            x_send.at[which, row],
            x_recv.at[which, row],
            to_group(g),
        )

    half_copy = remote(outs.at[0], outs.at[0], o_send, o_recv, sibling)

    def fold(row):
        for j in range(0, entries):
            block = jnp.dot(inv_v[row, 0], fac_v[row, 0, j], preferred_element_type=F32)
            blocks[0, row, j] = block.astype(BF16)

    def plan():
        load_size.wait()
        ends = []
        running = jnp.int32(0)
        for level in range(levels):
            running = running + size_ref[level]
            ends.append(running)

        def level_of(position):
            found = jnp.int32(0)
            for end in ends[:-1]:
                found = found + (position >= end).astype(jnp.int32)
            return found

        return level_of, [level_of(row * n_chain + me) for row in range(rows)]

    def times_inverse_t(row):
        return lax.dot_general(
            rhs_v[row, 0], inv_v[row, 0], (((1,), (1,)), ((), ())), preferred_element_type=F32
        )

    def drain(ref, start, count, sem):
        part = ref.at[pl.ds(start, count)]
        pltpu.make_async_copy(part, part, sem).wait()

    def less(half, parts):
        return (half.astype(F32) - tree([part.astype(F32) for part in parts])).astype(BF16)

    def times_inverse(value, row):
        return jnp.dot(value, inv_v[row, 0], preferred_element_type=F32).astype(BF16)

    later_levels = pl.ds(1, levels - 1)
    solved_copy = remote(
        sol_lv.at[later_levels], sol_lv.at[later_levels], v_send, v_recv, sibling
    )

    @pl.when(jnp.logical_not(is_worker))
    def _():
        pl.semaphore_signal(barrier, inc=1, device_id=sibling, device_id_type=MESH)
        start_loads()
        load_rhs.wait()
        load_inv.wait()
        load_fac.wait()
        fold(0)
        pl.semaphore_wait(barrier, groups)
        pats = [pat_to(1, sibling)] + [pat_to(2 * g + 1, to_group(g)) for g in range(1, groups)]
        for copy in pats:
            copy.start()
        to_sibling(0).start()
        for row in range(1, rows):
            fold(row)
            to_sibling(row).start()
        order = list(reversed(range(rows)))
        half = (rows + 1) // 2
        for part in (order[:half], order[half:]):
            for row in part:
                for g in range(1, groups):
                    across(g, 0, row).start()
            for row in part:
                to_helper(row).wait_recv()
                for g in range(1, groups):
                    across(g, 1, row).start()
        for copy in pats:
            copy.wait_send()
        for row in range(rows):
            to_sibling(row).wait_send()
            for g in range(1, groups):
                across(g, 0, row).wait_send()
                across(g, 1, row).wait_send()
        own_level = plan()[1]
        half = times_inverse_t(0).astype(BF16)
        half_copy.wait_recv()
        solved_copy.wait_recv()
        sol_lv[0] = half
        for r in range(rows):
            outs[1, r, 0] = sol_lv[own_level[r]]
        kept = outs[1, 0, 0]
        drain(brx.at[0], 0, n_chain, h_recv)
        value = less(half, [brx[0, d] for d in range(n_chain)])
        outs[1, 0, 0] = jnp.where(own_level[0] == 0, times_inverse(value, 0), kept)

    @pl.when(is_worker)
    def _():
        for d in chain_order:
            pl.semaphore_signal(barrier, inc=1, device_id=(lanes[d], k), device_id_type=MESH)
        for g in range(groups):
            if g:
                pl.semaphore_signal(barrier, inc=1, device_id=to_group(g), device_id_type=MESH)
            pl.semaphore_signal(
                barrier, inc=1, device_id=(me, columns[g] - 1), device_id_type=MESH
            )
        start_loads()
        own_pat = pltpu.make_async_copy(pat_hbm, pat_s.at[0], pat_sem.at[0])
        own_pat.start()

        load_rhs.wait()
        load_inv.wait()

        first = times_inverse_t(0)
        frx[0, 0] = first.astype(BF16)
        pl.semaphore_wait(barrier, n_chain + groups - 1)

        def share(level, whole):
            for d, g in [(d, 0) for d in chain_order] if whole else peers:
                remote(
                    frx.at[level, 0],
                    frx.at[level, g * n_chain + d],
                    f_send.at[level],
                    f_recv.at[level],
                    (lanes[d], columns[g]),
                ).start()

        def is_whole(level):
            return level == 0 or level >= first_full

        def copies(level):
            return (n_chain if is_whole(level) else n_chain * groups) - 1

        def candidates(level):
            return list(range(max(0, rows - levels + level), min(level, rows - 1) + 1))

        def picked(level, which, j, at):
            first_row, *others = candidates(level)
            block = blocks[which, first_row, j, at, :]
            for row in others:
                block = jnp.where(slot[level] == row, blocks[which, row, j, at, :], block)
            return block

        def fill_codes(whiches):
            for which in whiches:
                for row in range(rows):
                    for j in range(entries):
                        target = pat_s[which, row, 0, j]
                        code_s[which, row, j] = level_of(target) * n_chain + lax.rem(
                            target, n_chain
                        )

        def build(level, whiches, add):
            keys = [
                jnp.where(live[level], code_s[w, slot[level], j], -1) - (level - 1) * n_chain
                for w in whiches
                for j in range(entries)
            ]

            def chunk(i, carry):
                at = pl.ds(pl.multiple_of(i * STEP, STEP), STEP)
                found = [picked(level, w, j, at) for w in whiches for j in range(entries)]
                for d in range(n_chain):
                    parts = [
                        jnp.where(key == lanes[d], block, jnp.zeros_like(block))
                        for key, block in zip(keys, found)
                    ]
                    if add:
                        parts.append(dense[level - 1, d, at, :])
                    dense[level - 1, d, at, :] = tree(parts)
                return carry

            lax.fori_loop(0, width // STEP, chunk, 0)

        def turn(level):
            def one(d):
                at = pl.ds(d * width, width)
                dense_t[at, :] = dense[level - 1, d].astype(F32).T.astype(BF16)

            loop(n_chain, one)

        def older(level, whiches):
            sums = None
            for w in whiches:
                for j in range(0, entries, 2):
                    pair = range(j, min(j + 2, entries))
                    left = jnp.concatenate([store[code_s[w, slot[level], i]] for i in pair], axis=1)
                    right = jnp.concatenate(
                        [picked(level, w, i, pl.ds(0, width)) for i in pair], axis=1
                    )
                    term = lax.dot_general(
                        left, right, (((1,), (1,)), ((), ())), preferred_element_type=F32
                    )
                    sums = term if sums is None else sums + term
            return sums

        near = [0, 1]
        far = list(range(2, n_col))
        share(0, True)
        for g in range(1, groups):
            pl.semaphore_signal(ready, inc=1, device_id=to_group(g), device_id_type=MESH)

        level_of, own_level = plan()
        slot = []
        live = []
        for level in range(levels):
            here = jnp.int32(0)
            count = jnp.int32(0)
            for row in range(rows):
                match = own_level[row] == level
                here = jnp.where(match, row, here)
                count = count + match.astype(jnp.int32)
            slot.append(here)
            live.append(count > 0)

        load_fac.wait()
        for row in reversed(range(rows)):
            fold(row)
            to_helper(row).start()
        pats = [pat_to(2 * g, to_group(g)) for g in range(1, groups)]
        for copy in pats:
            copy.start()
        base[0] = first
        for row in range(1, rows):
            base[row] = times_inverse_t(row)
        store[...] = jnp.zeros_like(store)
        acc[...] = jnp.zeros_like(acc)
        own_pat.wait()
        pat_to(1, sibling).wait_recv()
        other_pat = pltpu.make_async_copy(pat_v.at[1], pat_s.at[1], pat_sem.at[1])
        other_pat.start()
        other_pat.wait()
        fill_codes(near)
        for row in range(rows):
            to_sibling(row).wait_recv()
        build(1, near, False)
        turn(1)
        if groups > 1:
            pl.semaphore_wait(ready, groups - 1)

        keep = (group == 0).astype(F32)
        for level in range(1, levels):
            whole = is_whole(level)
            before = base[slot[level]]
            if not whole:
                before = before * keep
            if level > 1:
                before = before - older(level, near + far if whole else near)
            drain(frx.at[level - 1], 1, copies(level - 1), f_recv.at[level - 1])
            found = []
            for d in range(n_chain):
                if is_whole(level - 1):
                    found.append(frx[level - 1, d])
                else:
                    parts = [frx[level - 1, g * n_chain + d].astype(F32) for g in range(groups)]
                    found.append(tree(parts).astype(BF16))
            sums = jnp.dot(
                jnp.concatenate(found, axis=1), dense_t[...], preferred_element_type=F32
            )
            value = (before - sums).astype(BF16)
            half_lv[level - 1] = found[0]
            if level == last:
                half_lv[level] = value
                break
            frx[level, 0] = value
            share(level, whole)
            for d in range(n_chain):
                store[(level - 1) * n_chain + lanes[d]] = found[d]
            if level + 1 == first_full:
                moved = []
                for which in far:
                    pat_to(which, sibling).wait_recv()
                    moved.append(
                        pltpu.make_async_copy(pat_v.at[which], pat_s.at[which], pat_sem.at[which])
                    )
                    moved[-1].start()
                for copy in moved:
                    copy.wait()
                fill_codes(far)
            if is_whole(level + 1):
                for which in far:
                    for row in candidates(level + 1):
                        if level + 1 == first_full:
                            remote(
                                blocks.at[which, row],
                                blocks.at[which, row],
                                x_send.at[which, row],
                                x_recv.at[which, row],
                                sibling,
                            ).wait_recv()
            build(level + 1, near + far if is_whole(level + 1) else near, False)
            turn(level + 1)

        arrived = set(candidates(first_full)) | set(candidates(last))
        for level in reversed(range(1, levels)):
            t = level - 1
            for d in reversed(range(0, n_chain, 2)):
                pair = jnp.concatenate([dense[t, d], dense[t, d + 1]], axis=1)
                both = jnp.dot(value, pair, preferred_element_type=F32)
                for i, part in ((1, both[:, width:]), (0, both[:, :width])):
                    message = (acc[t, d + i] + part).astype(BF16)
                    if d + i or t == 0:
                        btx[t, d + i] = message
                    if t == 0:
                        remote(
                            btx.at[t, d + i],
                            brx.at[t, d + i],
                            h_send,
                            h_recv,
                            (lanes[d + i], k - 1),
                        ).start()
                    if d + i:
                        remote(
                            btx.at[t, d + i],
                            brx.at[t, d + i],
                            b_send.at[t],
                            b_recv.at[t],
                            (lanes[d + i], k),
                        ).start()
                    else:
                        own = message
            sol_lv[level] = times_inverse(value, slot[level])
            if t == 0:
                sol_lv[0] = half_lv[0]
            if t == 0:
                solved_copy.start()
                for r in range(rows):
                    outs[1, r, 0] = sol_lv[own_level[r]]
                kept = outs[1, 0, 0]
                for i in range(last):
                    drain(frx.at[i], 1, copies(i), f_send.at[i])
                    if i:
                        drain(brx.at[i], 1, n_chain - 1, b_send.at[i])
                for row in range(rows):
                    to_helper(row).wait_send()
                for copy in pats:
                    copy.wait_send()
                half_copy.wait_send()
                solved_copy.wait_send()
            if level == last:
                for r in range(rows):
                    outs[0, r, 0] = half_lv[own_level[r]]
                half_copy.start()
            if t > 0:
                everything = near + far
                keys = []
                for w in everything:
                    for j in range(0, entries, 2):
                        pair = jnp.concatenate(
                            [picked(level, w, i, pl.ds(0, width)) for i in (j, j + 1)], axis=1
                        )
                        both = jnp.dot(value, pair, preferred_element_type=F32)
                        terms[w * entries + j] = both[:, :width]
                        terms[w * entries + j + 1] = both[:, width:]
                        for i in (j, j + 1):
                            keys.append(jnp.where(live[level], code_s[w, slot[level], i], -1))

                def later(target, carry):
                    for d in range(n_chain):
                        place = target * n_chain + lanes[d]
                        parts = [acc[target, d]] + [
                            jnp.where(key == place, terms[j], 0.0) for j, key in enumerate(keys)
                        ]
                        acc[target, d] = tree(parts)
                    return carry

                lax.fori_loop(0, t, later, 0)
                if not is_whole(t):
                    for row in candidates(t):
                        if row not in arrived:
                            arrived.add(row)
                            for which in far:
                                remote(
                                    blocks.at[which, row],
                                    blocks.at[which, row],
                                    x_send.at[which, row],
                                    x_recv.at[which, row],
                                    sibling,
                                ).wait_recv()
                    build(t, far, True)
            drain(brx.at[t], 1, n_chain - 1, b_recv.at[t])
            value = less(half_lv[t], [own] + [brx[t, d] for d in range(1, n_chain)])

        outs[1, 0, 0] = jnp.where(own_level[0] == 0, times_inverse(value, 0), kept)
        drain(brx.at[0], 1, n_chain - 1, b_send.at[0])
        drain(btx.at[0], 0, n_chain, h_send)


def per_device(n_chain, n_col, rhs, pattern, factor, inverse, level_size):
    rows, _, probes, width = rhs.shape
    entries = factor.shape[2]
    levels = level_size.shape[0]
    workers = n_chain * (n_col // 2)
    dma = pltpu.SemaphoreType.DMA
    vmem = pl.BlockSpec(memory_space=pltpu.VMEM)
    hbm = pl.BlockSpec(memory_space=pl.ANY)
    out = pltpu.VMEM((2,) + rhs.shape, rhs.dtype)
    both = pl.pallas_call(
        functools.partial(kernel, n_chain, n_col, levels),
        out_shape=out,
        in_specs=[hbm, hbm, hbm, hbm, hbm],
        out_specs=vmem,
        scratch_shapes=[
            pltpu.VMEM(rhs.shape, BF16),
            pltpu.VMEM(inverse.shape, BF16),
            pltpu.VMEM(factor.shape, BF16),
            pltpu.VMEM((n_col, rows, 1, entries), jnp.int32),
            pltpu.SMEM((n_col, rows, 1, entries), jnp.int32),
            pltpu.SMEM((n_col, rows, entries), jnp.int32),
            pltpu.VMEM((n_col, rows, entries, width, width), BF16),
            pltpu.VMEM((levels - 1, n_chain, width, width), BF16),
            pltpu.VMEM((n_chain * width, width), BF16),
            pltpu.VMEM((rows, probes, width), F32),
            pltpu.VMEM((levels * n_chain, probes, width), BF16),
            pltpu.VMEM((levels, workers, probes, width), BF16),
            pltpu.VMEM((levels, n_chain, probes, width), BF16),
            pltpu.VMEM((levels, n_chain, probes, width), BF16),
            pltpu.VMEM((levels, n_chain, probes, width), F32),
            pltpu.VMEM((n_col * entries, probes, width), F32),
            pltpu.VMEM((levels, probes, width), BF16),
            pltpu.VMEM((levels, probes, width), BF16),
            pltpu.SMEM((levels,), jnp.int32),
            dma((4,)),
            dma((n_col,)),
            dma((levels,)),
            dma((levels,)),
            dma((levels,)),
            dma((levels,)),
            dma((n_col,)),
            dma((n_col,)),
            dma((rows,)),
            dma((rows,)),
            dma((rows,)),
            dma((rows,)),
            dma((n_col, rows)),
            dma((n_col, rows)),
            dma,
            dma,
            dma,
            dma,
            dma,
            dma,
            pltpu.SemaphoreType.REGULAR,
        ],
        compiler_params=pltpu.CompilerParams(
            collective_id=0, has_side_effects=True, vmem_limit_bytes=56 * 1024 * 1024
        ),
    )(rhs, pattern, factor, inverse, level_size)
    return both[0], both[1]


def solution(mesh):
    return jax.shard_map(
        functools.partial(per_device, mesh.shape["chain"], mesh.shape["col"]),
        mesh=mesh,
        in_specs=(
            P(None, "chain", None, None),
            P(None, "chain", "col"),
            P(None, "chain", "col", None, None),
            P(None, "chain", None, None),
            P(),
        ),
        out_specs=(P(None, "chain", None, None), P(None, "chain", None, None)),
        check_vma=False,
    )
```
